32 devices in a mesh: chan: 4 (over y, core), inp: 8 (over z, x).
Axes of the slice: x: 2, y: 2, z: 4, core: 2. Of those that a mesh axis runs over, the one named last changes fastest.
Arguments:
- voltages: bfloat16 [1024, 131072], P('inp', 'chan'), may hold values from -64 to 64
- tile_table: int32 [40, 2], replicated, may hold values from -1 to 7, as said below
Outputs:
- coherence: float32 [512, 40, 128, 256], P('chan', 'inp')
The draws below stay inside these ranges and needn't reach their ends.
Inputs may be any that keep to these rules, and one draw needn't show every extreme that they name: `tile_table`: rows 5 d to 5 d + 4 are the slots whose tiles the device at index d along inp outputs. Every pair (a, b) with 0 <= a <= b < 8 stands in exactly one row, and every other row is (-1, -1); the pairs are spread over the rows in any order.
All inputs are finite; a program needn't handle non-finite values.
Results may differ from the reference program's by a relative error of at most 0.0058.
Values may be sent and summed in bfloat16 or wider, within the bound.
A program may use at most 256 MiB of HBM per device.

```python
import math
import jax
import jax.numpy as jnp
import numpy as np
from jax import lax

NI = 1024
L = 2048
NCH = 512
TAPS = 4
NB = 128
FRAMES = 64
NSAMP = 131072
N_INP = 8


def draw_voltages(key, part):
    key_noise = jax.random.fold_in(key, 0)
    thermal = jax.random.normal(key_noise, (NI, NSAMP), jnp.float32)
    values = thermal
    return jnp.clip(values, -64.0, 64.0).astype(jnp.bfloat16)


def draw_tile_table(key, part):
    tile_count = N_INP * (N_INP + 1) // 2
    slot_count = N_INP * (N_INP // 2 + 1)
    upper_rows, upper_cols = np.triu_indices(N_INP)
    pair_list = np.concatenate([np.stack([upper_rows, upper_cols], axis=1), -np.ones((slot_count - tile_count, 2), np.int64)], axis=0)
    pair_list = jnp.asarray(pair_list.astype(np.int32))
    shuffle = jax.random.permutation(key, slot_count)
    return pair_list[shuffle]


def setup_inputs(seed: int = 0) -> dict:
    keys = jax.random.split(jax.random.key(seed), 3)
    return {
        "voltages": draw_voltages(jax.random.fold_in(keys[2], 71), 0),
        "tile_table": draw_tile_table(jax.random.fold_in(keys[2], 71), 0),
    }


def filter_window():
    positions = jnp.arange(TAPS * L, dtype=jnp.float32)
    shape_sinc = jnp.sinc((positions - TAPS * L / 2.0) / L)
    tapering = 0.5 - 0.5 * jnp.cos(2.0 * math.pi * positions / (TAPS * L))
    return (shape_sinc * tapering).reshape(TAPS, L)

def transform_table():
    samples = jnp.arange(L, dtype=jnp.int32)[:, None]
    channels = jnp.arange(NCH, dtype=jnp.int32)[None, :]
    phases = samples * channels % L
    angles = phases.astype(jnp.float32) * (2.0 * math.pi / L)
    return jnp.stack([jnp.cos(angles), -jnp.sin(angles)], axis=2).reshape(L, 2 * NCH).astype(jnp.bfloat16)

def rotate_parts(rows):
    half_width = rows.shape[-1] // 2
    return jnp.concatenate([-rows[..., half_width:], rows[..., :half_width]], axis=-1)

def channel_tiles(columns, channel_power, first_all, second_all, present_all, block_width, frame_total):
    partner = jnp.concatenate([columns, rotate_parts(columns)], axis=0)
    gram_full = lax.dot_general(columns, partner, (((1,), (1,)), ((), ())), preferred_element_type=jnp.float32)
    block_count = columns.shape[0] // block_width
    gram_grid = gram_full.reshape(block_count, block_width, 2, block_count, block_width)
    picked = gram_grid[first_all, :, :, second_all, :]
    picked = picked.reshape(first_all.shape[0], block_width, 2 * block_width)
    power_grid = channel_power.reshape(block_count, block_width)
    inverse = present_all[:, None, None] / (frame_total * jnp.sqrt(power_grid[first_all][:, :, None] * power_grid[second_all][:, None, :]))
    return picked * jnp.concatenate([inverse, inverse], axis=2)

def reference(voltages, tile_table):
    blocks = voltages.reshape(NI, FRAMES, L)
    extended = jnp.concatenate([blocks, jnp.zeros((NI, TAPS - 1, L), voltages.dtype)], axis=1)
    window = filter_window()
    filtered = jnp.zeros((NI, FRAMES, L), jnp.float32)
    for tap_index in range(TAPS):
        filtered = filtered + extended[:, tap_index:tap_index + FRAMES, :].astype(jnp.float32) * window[tap_index]
    filtered = filtered.astype(jnp.bfloat16).reshape(NI * FRAMES, L)
    spectra = jnp.dot(filtered, transform_table(), preferred_element_type=jnp.float32).astype(jnp.bfloat16)
    arranged = spectra.reshape(NI, FRAMES, NCH, 2).transpose(2, 0, 3, 1).reshape(NCH, NI, 2 * FRAMES)
    autopower = lax.optimization_barrier(jnp.sum(jnp.square(arranged.astype(jnp.float32)), axis=2)) / FRAMES + 1e-06
    first_all = jnp.maximum(tile_table[:, 0], 0).astype(jnp.int32)
    second_all = jnp.maximum(tile_table[:, 1], 0).astype(jnp.int32)
    present_all = (tile_table[:, 0] >= 0).astype(jnp.float32)

    def per_channel(pair_in):
        return channel_tiles(pair_in[0], pair_in[1], first_all, second_all, present_all, NB, FRAMES)
    return lax.map(per_channel, (arranged, autopower))
```

```python
import functools
import math

import jax
import jax.numpy as jnp
from jax import lax
from jax.experimental import pallas as pl
from jax.experimental.pallas import tpu as pltpu
from jax.sharding import PartitionSpec as P

L = 2048
NCH = 512
TAPS = 4
FINE = 64
MESH = pl.DeviceIdType.MESH


def passed_along(array, axis, by):
    devices = lax.axis_size(axis)
    pairs = [(i, i + by) for i in range(devices) if 0 <= i + by < devices]
    return lax.ppermute(array, axis, pairs)


def filter_window():
    positions = jnp.arange(TAPS * L, dtype=jnp.float32)
    shape_sinc = jnp.sinc((positions - TAPS * L / 2.0) / L)
    tapering = 0.5 - 0.5 * jnp.cos(2.0 * math.pi * positions / (TAPS * L))
    return (shape_sinc * tapering).reshape(TAPS, L)


def turn_angles(samples):
    channels = jnp.arange(NCH, dtype=jnp.int32)[None, :]
    phases = samples[:, None] * channels % L
    angles = phases.astype(jnp.float32) * (2.0 * math.pi / L)
    return jnp.cos(angles), jnp.sin(angles)


def transform_table(groups):
    coarse_cos, coarse_sin = turn_angles(jnp.arange(L // FINE, dtype=jnp.int32) * FINE)
    fine_cos, fine_sin = turn_angles(jnp.arange(FINE, dtype=jnp.int32))
    coarse_cos, coarse_sin = coarse_cos[:, None, :], coarse_sin[:, None, :]
    fine_cos, fine_sin = fine_cos[None], fine_sin[None]
    real = (coarse_cos * fine_cos - coarse_sin * fine_sin).reshape(L, groups, 1, -1)
    imag = -(coarse_sin * fine_cos + coarse_cos * fine_sin).reshape(L, groups, 1, -1)
    return (
        jnp.concatenate([real.astype(jnp.bfloat16), imag.astype(jnp.bfloat16)], axis=2)
        .reshape(L, 2 * NCH)
    )


def channelize(voltages, groups):
    block_width, local_len = voltages.shape
    local_frames = local_len // L
    following = passed_along(voltages[:, : (TAPS - 1) * L], "chan", -1)
    extended = jnp.concatenate([voltages, following], axis=1).reshape(
        block_width, local_frames + TAPS - 1, L
    )
    window = filter_window()
    filtered = jnp.zeros((block_width, local_frames, L), jnp.float32)
    for tap_index in range(TAPS):
        filtered = (
            filtered
            + extended[:, tap_index : tap_index + local_frames, :].astype(jnp.float32)
            * window[tap_index]
        )
    filtered = filtered.astype(jnp.bfloat16).reshape(block_width * local_frames, L)
    spectra = jnp.dot(
        filtered, transform_table(groups), preferred_element_type=jnp.float32
    ).astype(jnp.bfloat16)
    return spectra.reshape(block_width, local_frames, 2 * NCH)


def arrange(turned):
    input_count, frame_total, column_count = turned.shape
    rows = (
        turned.reshape(input_count, frame_total, 2, column_count // 2)
        .transpose(3, 0, 2, 1)
        .reshape(column_count // 2, input_count, 2 * frame_total)
    ).astype(jnp.float32)
    autopower = jnp.sum(jnp.square(rows), axis=2, keepdims=True) / frame_total + 1e-06
    return (rows / (math.sqrt(frame_total) * jnp.sqrt(autopower))).astype(jnp.bfloat16)


def gather_kernel(sizes, own_ref, all_ref, stage, send_line, send_cross, recv_sem, local_sem):
    rows, columns, chunks, crossed = sizes
    step = own_ref.shape[0] // chunks
    me = lax.axis_index("inp")
    z, x = lax.div(me, columns), lax.rem(me, columns)
    up = ("up", 0, z < rows - 1, me + columns)
    down = ("down", 1, z > 0, me - columns)
    right = ("right", 2, x < columns - 1, me + 1)
    left = ("left", 3, x > 0, me - 1)
    along_z, along_x = (up, down), (right, left)

    barrier = pltpu.get_barrier_semaphore()
    expected = jnp.int32(0)
    for _, _, exists, target in along_z + along_x:
        expected = expected + exists.astype(jnp.int32)

        @pl.when(exists)
        def _(target=target):
            pl.semaphore_signal(barrier, inc=1, device_id={"inp": target}, device_id_type=MESH)

    pl.semaphore_wait(barrier, expected)

    def part(ref, chunk):
        return ref.at[pl.ds(chunk * step, step)]

    def copy(source, block, chunk, way, sems):
        return pltpu.make_async_remote_copy(
            src_ref=part(source, chunk),
            dst_ref=part(all_ref.at[block], chunk),
            send_sem=sems.at[way[1], block],
            recv_sem=recv_sem.at[block, chunk],
            device_id={"inp": way[3]},
            device_id_type=MESH,
        )

    def send(source, block, chunk, ways, sems):
        for way in ways:

            @pl.when(way[2])
            def _(way=way):
                copy(source, block, chunk, way, sems).start()

    def pass_on(block, chunk, exists, ways, sems, origin):
        @pl.when(exists)
        def _():
            copy(all_ref.at[block], block, chunk, origin, sems).wait_recv()
            send(all_ref.at[block], block, chunk, ways, sems)

    def over(first, last, body):
        def one(chunk, carry):
            body(chunk)
            return carry

        lax.fori_loop(first, last, one, jnp.int32(0))

    over(0, crossed, lambda c: send(own_ref, me, c, along_x + along_z, send_cross))
    over(crossed, chunks, lambda c: send(own_ref, me, c, along_z + along_x, send_line))
    load = pltpu.make_async_copy(own_ref, stage, local_sem.at[0])
    load.start()
    load.wait()
    store = pltpu.make_async_copy(stage, all_ref.at[me], local_sem.at[1])
    store.start()

    for away in range(1, columns):
        over(
            0,
            crossed,
            lambda c: (
                pass_on(me - away, c, x >= away, (right,) + along_z, send_cross, left),
                pass_on(me + away, c, x + away < columns, (left,) + along_z, send_cross, right),
            ),
        )
    for away in range(1, rows):
        below, above = z >= away, z + away < rows
        over(
            crossed,
            chunks,
            lambda c: (
                pass_on(me - away * columns, c, below, along_x + (up,), send_line, down),
                pass_on(me + away * columns, c, above, along_x + (down,), send_line, up),
            ),
        )
        for column in range(columns):
            low = (z - away) * columns + column
            high = (z + away) * columns + column
            over(
                0,
                crossed,
                lambda c: (
                    pass_on(low, c, below, (up,), send_cross, down),
                    pass_on(high, c, above, (down,), send_cross, up),
                ),
            )
    for away in range(1, columns):
        for row in range(rows):
            before = row * columns + x - away
            after = row * columns + x + away
            over(
                crossed,
                chunks,
                lambda c: (
                    pass_on(before, c, x >= away, (right,), send_line, left),
                    pass_on(after, c, x + away < columns, (left,), send_line, right),
                ),
            )

    def drain(block, way, cond, sems, first, count):
        @pl.when(jnp.logical_and(cond, way[2]))
        def _():
            whole = all_ref.at[block, pl.ds(first * step, count * step)]
            pltpu.make_async_remote_copy(
                src_ref=whole,
                dst_ref=whole,
                send_sem=sems.at[way[1], block],
                recv_sem=recv_sem.at[block, 0],
                device_id={"inp": way[3]},
                device_id_type=MESH,
            ).wait_send()

    for row in range(rows):
        for column in range(columns):
            block = row * columns + column
            plain, turned = chunks - crossed, crossed
            here = x == column
            drain(block, up, jnp.logical_and(here, z >= row), send_line, crossed, plain)
            drain(block, down, jnp.logical_and(here, z <= row), send_line, crossed, plain)
            drain(block, right, x >= column, send_line, crossed, plain)
            drain(block, left, x <= column, send_line, crossed, plain)
            if turned:
                same = z == row
                drain(block, up, z >= row, send_cross, 0, turned)
                drain(block, down, z <= row, send_cross, 0, turned)
                drain(block, right, jnp.logical_and(same, x >= column), send_cross, 0, turned)
                drain(block, left, jnp.logical_and(same, x <= column), send_cross, 0, turned)
    store.wait()


def gather(own):
    devices = lax.axis_size("inp")
    columns = 1 << (int(math.log2(devices)) // 2)
    rows = devices // columns
    chunks = 8
    crossed = 1
    return pl.pallas_call(
        functools.partial(gather_kernel, (rows, columns, chunks, crossed)),
        out_shape=jax.ShapeDtypeStruct((devices,) + own.shape, own.dtype),
        in_specs=[pl.BlockSpec(memory_space=pl.ANY)],
        out_specs=pl.BlockSpec(memory_space=pl.ANY),
        scratch_shapes=[
            pltpu.VMEM(own.shape, own.dtype),
            pltpu.SemaphoreType.DMA((4, devices)),
            pltpu.SemaphoreType.DMA((4, devices)),
            pltpu.SemaphoreType.DMA((devices, chunks)),
            pltpu.SemaphoreType.DMA((2,)),
        ],
        compiler_params=pltpu.CompilerParams(collective_id=0, has_side_effects=True),
        name="gather",
    )(own)


def tile_kernel(slots, table_ref, all_ref, out_ref):
    def one(channel, carry):
        for slot in range(slots):
            first, second = table_ref[slot, 0], table_ref[slot, 1]
            present = first >= 0

            @pl.when(present)
            def _(slot=slot, first=first, second=second):
                left = all_ref[first, channel]
                right = all_ref[second, channel]
                half = right.shape[1] // 2
                turned = jnp.concatenate([-right[:, half:], right[:, :half]], axis=1)
                partner = jnp.concatenate([right, turned], axis=0)
                out_ref[channel, slot] = lax.dot_general(
                    left,
                    partner,
                    (((1,), (1,)), ((), ())),
                    preferred_element_type=jnp.float32,
                )

            @pl.when(jnp.logical_not(present))
            def _(slot=slot):
                out_ref[channel, slot] = jnp.zeros(out_ref.shape[2:], jnp.float32)

        return carry

    lax.fori_loop(0, all_ref.shape[1], one, jnp.int32(0), unroll=2)


def make_tiles(everything, slot_rows):
    devices, channel_count, block_width, depth = everything.shape
    slots = slot_rows.shape[0]
    group = 8
    return pl.pallas_call(
        functools.partial(tile_kernel, slots),
        out_shape=jax.ShapeDtypeStruct(
            (channel_count, slots, block_width, 2 * block_width), jnp.float32
        ),
        grid_spec=pltpu.PrefetchScalarGridSpec(
            num_scalar_prefetch=1,
            grid=(channel_count // group,),
            in_specs=[
                pl.BlockSpec((devices, group, block_width, depth), lambda c, t: (0, c, 0, 0))
            ],
            out_specs=pl.BlockSpec(
                (group, slots, block_width, 2 * block_width), lambda c, t: (c, 0, 0, 0)
            ),
        ),
        compiler_params=pltpu.CompilerParams(vmem_limit_bytes=56 << 20),
        name="tiles",
    )(slot_rows, everything)


def on_device(voltages, tile_table):
    spectra = channelize(voltages, lax.axis_size("chan"))
    turned = lax.all_to_all(spectra, "chan", split_axis=2, concat_axis=1, tiled=True)
    everything = gather(arrange(turned))
    slot_total = tile_table.shape[0] // lax.axis_size("inp")
    slot_rows = lax.dynamic_slice_in_dim(
        tile_table, lax.axis_index("inp") * slot_total, slot_total, 0
    )
    return make_tiles(everything, slot_rows)


def solution(mesh):
    placed = (P("inp", "chan"), P())
    return jax.shard_map(
        on_device,
        mesh=mesh,
        in_specs=placed,
        out_specs=P("chan", "inp", None, None),
        check_vma=False,
    )
```

```python
import functools
import math

import jax
import jax.numpy as jnp
from jax import lax
from jax.experimental import pallas as pl
from jax.experimental.pallas import tpu as pltpu
from jax.sharding import PartitionSpec as P

L = 2048
NCH = 512
TAPS = 4
FINE = 64
PAIR = 2
MESH = pl.DeviceIdType.MESH


def filter_window():
    positions = jnp.arange(TAPS * L, dtype=jnp.float32)
    shape_sinc = jnp.sinc((positions - TAPS * L / 2.0) / L)
    tapering = 0.5 - 0.5 * jnp.cos(2.0 * math.pi * positions / (TAPS * L))
    return (shape_sinc * tapering).reshape(TAPS, L)


def turn_angles(rows, samples, quarter):
    channels, parts = rows // 2, rows % 2
    phases = (channels[:, None] * samples[None, :] + quarter * parts[:, None]) % L
    angles = phases.astype(jnp.float32) * (2.0 * math.pi / L)
    return jnp.cos(angles), jnp.sin(angles)


def transform_table():
    rows = jnp.arange(2 * NCH, dtype=jnp.int32)
    coarse_cos, coarse_sin = turn_angles(rows, jnp.arange(L // FINE, dtype=jnp.int32) * FINE, 0)
    fine_cos, fine_sin = turn_angles(rows, jnp.arange(L, dtype=jnp.int32)[:FINE], L // 4)
    spread = lambda values: jnp.repeat(values, FINE, axis=1)
    copied = lambda values: jnp.tile(values, (1, L // FINE))
    return (
        spread(coarse_cos) * copied(fine_cos) - spread(coarse_sin) * copied(fine_sin)
    ).astype(jnp.bfloat16)


def channel_kernel(groups, volt_ref, table_ref, window_ref, out_ref, *scratch):
    extended, filtered, total, load_sem, send_sem, recv_sem = scratch
    width, local_len = volt_ref.shape
    frames = local_len // L
    halo_len = (TAPS - 1) * L
    me = lax.axis_index("chan")
    has_next, has_last = me < groups - 1, me > 0

    load = pltpu.make_async_copy(volt_ref, extended.at[:, pl.ds(0, local_len)], load_sem)
    load.start()
    barrier = pltpu.get_barrier_semaphore()
    for exists, target in ((has_next, me + 1), (has_last, me - 1)):

        @pl.when(exists)
        def _(target=target):
            pl.semaphore_signal(barrier, inc=1, device_id={"chan": target}, device_id_type=MESH)

    pl.semaphore_wait(barrier, has_next.astype(jnp.int32) + has_last.astype(jnp.int32))
    halo = pltpu.make_async_remote_copy(
        src_ref=volt_ref.at[:, pl.ds(0, halo_len)],
        dst_ref=extended.at[:, pl.ds(local_len, halo_len)],
        send_sem=send_sem,
        recv_sem=recv_sem,
        device_id={"chan": me - 1},
        device_id_type=MESH,
    )

    @pl.when(has_last)
    def _():
        halo.start()

    @pl.when(jnp.logical_not(has_next))
    def _():
        extended[:, pl.ds(local_len, halo_len)] = jnp.zeros((width, halo_len), jnp.bfloat16)

    load.wait()
    strip, lanes = 16, 512

    def one_pair(pair):
        for inner in range(PAIR):
            frame = pair * PAIR + inner
            for first in range(0, L, lanes):
                weights = [
                    window_ref[tap : tap + 1, first : first + lanes] for tap in range(TAPS)
                ]

                def one_strip(index, carry):
                    rows = pl.ds(pl.multiple_of(index * strip, strip), strip)
                    value = jnp.zeros((strip, lanes), jnp.float32)
                    for tap in range(TAPS):
                        start = pl.multiple_of((frame + tap) * L + first, 128)
                        value = value + (
                            extended[rows, pl.ds(start, lanes)].astype(jnp.float32) * weights[tap]
                        )
                    to = pl.ds(pl.multiple_of(inner * width + index * strip, strip), strip)
                    filtered[to, first : first + lanes] = value.astype(jnp.bfloat16)
                    return carry

                lax.fori_loop(0, width // strip, one_strip, jnp.int32(0), unroll=2)
        step = min(256, 2 * NCH)
        for row in range(0, 2 * NCH, step):
            product = lax.dot_general(
                table_ref[row : row + step, :],
                filtered[...],
                (((1,), (1,)), ((), ())),
                preferred_element_type=jnp.float32,
            )
            for inner in range(PAIR):
                where = pl.ds(row * frames + pair * PAIR + inner, step, stride=frames)
                total[where, :] = product[:, inner * width : (inner + 1) * width]

    def pairs(first, last):
        def one(pair, carry):
            one_pair(pair)
            return carry

        lax.fori_loop(first, last, one, jnp.int32(0))

    clear = max(0, (frames - TAPS + 1) // PAIR)
    pairs(0, clear)

    @pl.when(has_next)
    def _():
        halo.wait_recv()

    pairs(clear, frames // PAIR)

    def put(index, carry):
        rows = pl.ds(pl.multiple_of(index * 256, 256), 256)
        out_ref[rows, :] = total[rows, :].astype(jnp.bfloat16)
        return carry

    lax.fori_loop(0, out_ref.shape[0] // 256, put, jnp.int32(0))

    @pl.when(has_last)
    def _():
        halo.wait_send()


def channelize(voltages):
    width, local_len = voltages.shape
    frames = local_len // L
    in_vmem = pl.BlockSpec(memory_space=pltpu.VMEM)
    spectra = pl.pallas_call(
        functools.partial(channel_kernel, lax.axis_size("chan")),
        out_shape=jax.ShapeDtypeStruct((2 * NCH * frames, width), jnp.bfloat16),
        in_specs=[pl.BlockSpec(memory_space=pl.ANY), in_vmem, in_vmem],
        out_specs=in_vmem,
        scratch_shapes=[
            pltpu.VMEM((width, local_len + (TAPS - 1) * L), jnp.bfloat16),
            pltpu.VMEM((PAIR * width, L), jnp.bfloat16),
            pltpu.VMEM((2 * NCH * frames, width), jnp.float32),
            pltpu.SemaphoreType.DMA,
            pltpu.SemaphoreType.DMA,
            pltpu.SemaphoreType.DMA,
        ],
        compiler_params=pltpu.CompilerParams(
            collective_id=1, has_side_effects=True, vmem_limit_bytes=56 << 20
        ),
        name="channels",
    )(voltages, transform_table(), filter_window())
    return spectra.reshape(NCH, 2 * frames, width)


def flipped(group, mask, groups):
    result, bit = group, 1
    while bit < groups:
        result = result + (mask // bit % 2) * bit * (1 - 2 * (group // bit % 2))
        bit *= 2
    return result


HALVES = 2


def gather_kernel(sizes, own_ref, all_ref, stage, *sems):
    rows, columns, groups = sizes
    send_line, send_cross, recv_sem, turn_send, turn_recv, local_sem = sems
    channels, depth = own_ref.shape[0] // groups, own_ref.shape[1]
    step = channels // HALVES
    chunks = groups * HALVES
    me, group = lax.axis_index("inp"), lax.axis_index("chan")
    z, x = me // columns, me % columns
    up = ("up", 0, z < rows - 1, me + columns)
    down = ("down", 1, z > 0, me - columns)
    right = ("right", 2, x < columns - 1, me + 1)
    left = ("left", 3, x > 0, me - 1)
    along_z, along_x = (up, down), (right, left)

    barrier = pltpu.get_barrier_semaphore()
    expected = jnp.int32(groups - 1)
    for mask in range(1, groups):
        target = flipped(group, mask, groups)
        pl.semaphore_signal(barrier, inc=1, device_id={"chan": target}, device_id_type=MESH)
    for _, _, exists, target in along_z + along_x:
        expected = expected + exists.astype(jnp.int32)

        @pl.when(exists)
        def _(target=target):
            pl.semaphore_signal(barrier, inc=1, device_id={"inp": target}, device_id_type=MESH)

    pl.semaphore_wait(barrier, expected)

    def part(block, chunk, sender):
        time = flipped(sender, chunk // HALVES, groups)
        return all_ref.at[
            block, pl.ds(chunk % HALVES * step, step), pl.ds(pl.multiple_of(time * depth, depth), depth)
        ]

    def own_part(to, half):
        return own_ref.at[pl.ds(to * channels + half * step, step)]

    def turn(chunk, arriving=False):
        target = flipped(group, chunk // HALVES, groups)
        return pltpu.make_async_remote_copy(
            src_ref=own_part(target, chunk % HALVES),
            dst_ref=part(me, chunk if arriving else chunk % HALVES, group),
            send_sem=turn_send.at[chunk],
            recv_sem=turn_recv.at[chunk],
            device_id={"chan": target},
            device_id_type=MESH,
        )

    def copy(block, chunk, way, to_sems, source=None):
        place = part(block, chunk, group)
        return pltpu.make_async_remote_copy(
            src_ref=place if source is None else source,
            dst_ref=place,
            send_sem=to_sems.at[way[1], block],
            recv_sem=recv_sem.at[block, chunk],
            device_id={"inp": way[3]},
            device_id_type=MESH,
        )

    def send(block, chunk, ways, to_sems, source=None):
        for way in ways:

            @pl.when(way[2])
            def _(way=way):
                copy(block, chunk, way, to_sems, source).start()

    def pass_on(block, chunk, exists, ways, to_sems, origin):
        @pl.when(exists)
        def _():
            copy(block, chunk, origin, to_sems).wait_recv()
            send(block, chunk, ways, to_sems)

    def over(first, last, body):
        def one(chunk, carry):
            body(chunk)
            return carry

        lax.fori_loop(first, last, one, jnp.int32(0))

    over(HALVES, chunks, lambda c: turn(c).start())
    send(me, 0, along_x + along_z, send_cross, own_part(group, 0))
    over(1, HALVES, lambda c: send(me, c, along_z + along_x, send_line, own_part(group, c)))
    load = pltpu.make_async_copy(own_ref.at[pl.ds(group * channels, channels)], stage, local_sem.at[0])
    load.start()
    load.wait()
    store = pltpu.make_async_copy(
        stage,
        all_ref.at[me, :, pl.ds(pl.multiple_of(group * depth, depth), depth)],
        local_sem.at[1],
    )
    store.start()

    def own_turned(mask):
        def one(chunk):
            turn(chunk, True).wait_recv()
            send(me, chunk, along_z + along_x, send_line)

        over(mask * HALVES, (mask + 1) * HALVES, one)

    def line(away, first, last):
        below, above = z >= away, z + away < rows

        def one(chunk):
            pass_on(me - away * columns, chunk, below, along_x + (up,), send_line, down)
            pass_on(me + away * columns, chunk, above, along_x + (down,), send_line, up)

        over(first, last, one)

    def crossing(away):
        below, above = z >= away, z + away < rows
        for column in range(columns):
            low = (z - away) * columns + column
            high = (z + away) * columns + column
            pass_on(low, 0, below, (up,), send_cross, down)
            pass_on(high, 0, above, (down,), send_cross, up)

    for away in range(1, columns):
        pass_on(me - away, 0, x >= away, (right,) + along_z, send_cross, left)
        pass_on(me + away, 0, x + away < columns, (left,) + along_z, send_cross, right)
    own_turned(1)
    crossing(1)
    line(1, 1, HALVES)
    for mask in range(2, groups):
        own_turned(mask)
        line(1, (mask - 1) * HALVES, mask * HALVES)
    line(1, chunks - HALVES, chunks)
    for away in range(2, rows):
        crossing(away)
        line(away, 1, chunks)
    for away in range(1, columns):
        for row in range(rows):
            before = row * columns + x - away
            after = row * columns + x + away

            def across(chunk):
                pass_on(before, chunk, x >= away, (right,), send_line, left)
                pass_on(after, chunk, x + away < columns, (left,), send_line, right)

            over(1, chunks, across)

    def drain(block, way, cond, to_sems, count):
        @pl.when(jnp.logical_and(cond, way[2]))
        def _():
            whole = all_ref.at[block, pl.ds(0, count * (channels // chunks))]
            pltpu.make_async_remote_copy(
                src_ref=whole,
                dst_ref=whole,
                send_sem=to_sems.at[way[1], block],
                recv_sem=recv_sem.at[block, 0],
                device_id={"inp": way[3]},
                device_id_type=MESH,
            ).wait_send()

    for row in range(rows):
        for column in range(columns):
            block = row * columns + column
            here, same = x == column, z == row
            drain(block, up, jnp.logical_and(here, z >= row), send_line, chunks - 1)
            drain(block, down, jnp.logical_and(here, z <= row), send_line, chunks - 1)
            drain(block, right, x >= column, send_line, chunks - 1)
            drain(block, left, x <= column, send_line, chunks - 1)
            drain(block, up, z >= row, send_cross, 1)
            drain(block, down, z <= row, send_cross, 1)
            drain(block, right, jnp.logical_and(same, x >= column), send_cross, 1)
            drain(block, left, jnp.logical_and(same, x <= column), send_cross, 1)
    over(HALVES, chunks, lambda c: turn(c).wait_send())
    store.wait()


def gather(spectra):
    devices, groups = lax.axis_size("inp"), lax.axis_size("chan")
    columns = 1 << (int(math.log2(devices)) // 2)
    rows = devices // columns
    channels, depth, width = spectra.shape[0] // groups, spectra.shape[1], spectra.shape[2]
    chunks = groups * HALVES
    return pl.pallas_call(
        functools.partial(gather_kernel, (rows, columns, groups)),
        out_shape=jax.ShapeDtypeStruct((devices, channels, groups * depth, width), spectra.dtype),
        in_specs=[pl.BlockSpec(memory_space=pl.ANY)],
        out_specs=pl.BlockSpec(memory_space=pl.ANY),
        scratch_shapes=[
            pltpu.VMEM((channels, depth, width), spectra.dtype),
            pltpu.SemaphoreType.DMA((4, devices)),
            pltpu.SemaphoreType.DMA((4, devices)),
            pltpu.SemaphoreType.DMA((devices, chunks)),
            pltpu.SemaphoreType.DMA((chunks,)),
            pltpu.SemaphoreType.DMA((chunks,)),
            pltpu.SemaphoreType.DMA((2,)),
        ],
        compiler_params=pltpu.CompilerParams(collective_id=0, has_side_effects=True),
        name="gather",
    )(spectra)


def tile_kernel(slots, frames, groups, table_ref, all_ref, out_ref):
    depth = all_ref.shape[2]
    local = depth // (2 * groups)

    def scaled(block, channel):
        rows = all_ref[block, channel].astype(jnp.float32)
        autopower = jnp.sum(rows * rows, axis=0, keepdims=True) / frames + 1e-06
        return rows * (1.0 / (math.sqrt(frames) * jnp.sqrt(autopower)))

    def one(channel, carry):
        for slot in range(slots):
            first, second = table_ref[slot, 0], table_ref[slot, 1]
            left = scaled(jnp.maximum(first, 0), channel)
            left = jnp.where(first >= 0, left, jnp.zeros_like(left)).astype(jnp.bfloat16)
            right = scaled(jnp.maximum(second, 0), channel).astype(jnp.bfloat16)
            pieces = []
            for start in range(0, depth, 2 * local):
                pieces.append(-right[start + local : start + 2 * local])
                pieces.append(right[start : start + local])
            partner = jnp.concatenate([right, jnp.concatenate(pieces, axis=0)], axis=1)
            out_ref[channel, slot] = lax.dot_general(
                left, partner, (((0,), (0,)), ((), ())), preferred_element_type=jnp.float32
            )
        return carry

    lax.fori_loop(0, all_ref.shape[1], one, jnp.int32(0), unroll=2)


def make_tiles(everything, slot_rows):
    devices, channel_count, depth, width = everything.shape
    slots = slot_rows.shape[0]
    group = 8
    return pl.pallas_call(
        functools.partial(tile_kernel, slots, depth // 2, lax.axis_size("chan")),
        out_shape=jax.ShapeDtypeStruct((channel_count, slots, width, 2 * width), jnp.float32),
        grid_spec=pltpu.PrefetchScalarGridSpec(
            num_scalar_prefetch=1,
            grid=(channel_count // group,),
            in_specs=[pl.BlockSpec((devices, group, depth, width), lambda c, t: (0, c, 0, 0))],
            out_specs=pl.BlockSpec((group, slots, width, 2 * width), lambda c, t: (c, 0, 0, 0)),
        ),
        compiler_params=pltpu.CompilerParams(vmem_limit_bytes=56 << 20),
        name="tiles",
    )(slot_rows, everything)


def on_device(voltages, tile_table):
    everything = gather(channelize(voltages))
    slot_total = tile_table.shape[0] // lax.axis_size("inp")
    slot_rows = lax.dynamic_slice_in_dim(
        tile_table, lax.axis_index("inp") * slot_total, slot_total, 0
    )
    return make_tiles(everything, slot_rows)


def solution(mesh):
    placed = (P("inp", "chan"), P())
    return jax.shard_map(
        on_device,
        mesh=mesh,
        in_specs=placed,
        out_specs=P("chan", "inp", None, None),
        check_vma=False,
    )
```

```python
import functools
import math

import jax
import jax.numpy as jnp
from jax import lax
from jax.experimental import pallas as pl
from jax.experimental.pallas import tpu as pltpu
from jax.sharding import PartitionSpec as P

L = 2048
NCH = 512
TAPS = 4
FINE = 128
PAIR = 2
MESH = pl.DeviceIdType.MESH


def filter_window():
    positions = jnp.arange(TAPS * L, dtype=jnp.float32)
    shape_sinc = jnp.sinc((positions - TAPS * L / 2.0) / L)
    tapering = 0.5 - 0.5 * jnp.cos(2.0 * math.pi * positions / (TAPS * L))
    return (shape_sinc * tapering).reshape(TAPS, L)


def turn_angles(rows, samples, quarter):
    channels, parts = rows // 2, rows % 2
    phases = (channels[:, None] * samples[None, :] + quarter * parts[:, None]) % L
    angles = phases.astype(jnp.float32) * (2.0 * math.pi / L)
    return jnp.cos(angles), jnp.sin(angles)


def table_factors():
    rows = jnp.arange(2 * NCH, dtype=jnp.int32)
    coarse = turn_angles(rows, jnp.arange(L // FINE, dtype=jnp.int32) * FINE, 0)
    fine = turn_angles(rows, jnp.arange(L, dtype=jnp.int32)[:FINE], L // 4)
    return coarse + fine


def fill_table(factors, table):
    coarse_cos, coarse_sin, fine_cos, fine_sin = factors
    strip = 128

    def one(index, carry):
        rows = pl.ds(pl.multiple_of(index * strip, strip), strip)
        cosines, sines = fine_cos[rows, :], fine_sin[rows, :]
        for column in range(L // FINE):
            table[rows, column * FINE : (column + 1) * FINE] = (
                coarse_cos[rows, column : column + 1] * cosines
                - coarse_sin[rows, column : column + 1] * sines
            ).astype(jnp.bfloat16)
        return carry

    lax.fori_loop(0, table.shape[0] // strip, one, jnp.int32(0))


def channel_kernel(groups, volt_ref, *refs):
    factors, window_ref, out_ref, scratch = refs[:4], refs[4], refs[5], refs[6:]
    extended, filtered, table_ref, total, load_sem, send_sem, recv_sem = scratch
    width, local_len = volt_ref.shape
    frames = local_len // L
    halo_len = (TAPS - 1) * L
    me = lax.axis_index("chan")
    has_next, has_last = me < groups - 1, me > 0

    load = pltpu.make_async_copy(volt_ref, extended.at[:, pl.ds(0, local_len)], load_sem)
    load.start()
    barrier = pltpu.get_barrier_semaphore()
    for exists, target in ((has_next, me + 1), (has_last, me - 1)):

        @pl.when(exists)
        def _(target=target):
            pl.semaphore_signal(barrier, inc=1, device_id={"chan": target}, device_id_type=MESH)

    pl.semaphore_wait(barrier, has_next.astype(jnp.int32) + has_last.astype(jnp.int32))
    halo = pltpu.make_async_remote_copy(
        src_ref=volt_ref.at[:, pl.ds(0, halo_len)],
        dst_ref=extended.at[:, pl.ds(local_len, halo_len)],
        send_sem=send_sem,
        recv_sem=recv_sem,
        device_id={"chan": me - 1},
        device_id_type=MESH,
    )

    @pl.when(has_last)
    def _():
        halo.start()

    @pl.when(jnp.logical_not(has_next))
    def _():
        extended[:, pl.ds(local_len, halo_len)] = jnp.zeros((width, halo_len), jnp.bfloat16)

    fill_table(factors, table_ref)
    load.wait()
    strip, lanes = 16, 512

    def one_pair(pair):
        for inner in range(PAIR):
            frame = pair * PAIR + inner
            for first in range(0, L, lanes):
                weights = [
                    window_ref[tap : tap + 1, first : first + lanes] for tap in range(TAPS)
                ]

                def one_strip(index, carry):
                    rows = pl.ds(pl.multiple_of(index * strip, strip), strip)
                    value = jnp.zeros((strip, lanes), jnp.float32)
                    for tap in range(TAPS):
                        start = pl.multiple_of((frame + tap) * L + first, 128)
                        value = value + (
                            extended[rows, pl.ds(start, lanes)].astype(jnp.float32) * weights[tap]
                        )
                    to = pl.ds(pl.multiple_of(inner * width + index * strip, strip), strip)
                    filtered[to, first : first + lanes] = value.astype(jnp.bfloat16)
                    return carry

                lax.fori_loop(0, width // strip, one_strip, jnp.int32(0), unroll=2)
        step = min(256, 2 * NCH)
        for row in range(0, 2 * NCH, step):
            product = lax.dot_general(
                table_ref[row : row + step, :],
                filtered[...],
                (((1,), (1,)), ((), ())),
                preferred_element_type=jnp.float32,
            )
            for inner in range(PAIR):
                where = pl.ds(row * frames + pair * PAIR + inner, step, stride=frames)
                total[where, :] = product[:, inner * width : (inner + 1) * width]

    def pairs(first, last):
        def one(pair, carry):
            one_pair(pair)
            return carry

        lax.fori_loop(first, last, one, jnp.int32(0))

    clear = max(0, (frames - TAPS + 1) // PAIR)
    pairs(0, clear)

    @pl.when(has_next)
    def _():
        halo.wait_recv()

    pairs(clear, frames // PAIR)

    def put(index, carry):
        rows = pl.ds(pl.multiple_of(index * 256, 256), 256)
        out_ref[rows, :] = total[rows, :].astype(jnp.bfloat16)
        return carry

    lax.fori_loop(0, out_ref.shape[0] // 256, put, jnp.int32(0))

    @pl.when(has_last)
    def _():
        halo.wait_send()


def channelize(voltages):
    width, local_len = voltages.shape
    frames = local_len // L
    in_vmem = pl.BlockSpec(memory_space=pltpu.VMEM)
    spectra = pl.pallas_call(
        functools.partial(channel_kernel, lax.axis_size("chan")),
        out_shape=jax.ShapeDtypeStruct((2 * NCH * frames, width), jnp.bfloat16),
        in_specs=[pl.BlockSpec(memory_space=pl.ANY)] + [in_vmem] * 5,
        out_specs=in_vmem,
        scratch_shapes=[
            pltpu.VMEM((width, local_len + (TAPS - 1) * L), jnp.bfloat16),
            pltpu.VMEM((PAIR * width, L), jnp.bfloat16),
            pltpu.VMEM((2 * NCH, L), jnp.bfloat16),
            pltpu.VMEM((2 * NCH * frames, width), jnp.float32),
            pltpu.SemaphoreType.DMA,
            pltpu.SemaphoreType.DMA,
            pltpu.SemaphoreType.DMA,
        ],
        compiler_params=pltpu.CompilerParams(
            collective_id=1, has_side_effects=True, vmem_limit_bytes=56 << 20
        ),
        name="channels",
    )(voltages, *table_factors(), filter_window())
    return spectra.reshape(NCH, 2 * frames, width)


def flipped(group, mask, groups):
    result, bit = group, 1
    while bit < groups:
        result = result + (mask // bit % 2) * bit * (1 - 2 * (group // bit % 2))
        bit *= 2
    return result


PARTS = 4


def gather_kernel(sizes, own_ref, all_ref, stage, *sems):
    rows, columns, groups, crossed = sizes
    send_line, send_cross, recv_sem, turn_send, turn_recv, local_sem = sems
    channels, depth = own_ref.shape[0] // groups, own_ref.shape[1]
    step = channels // PARTS
    chunks = 2 + (groups - 1) * PARTS
    me, group = lax.axis_index("inp"), lax.axis_index("chan")
    z, x = me // columns, me % columns
    up = ("up", 0, z < rows - 1, me + columns)
    down = ("down", 1, z > 0, me - columns)
    right = ("right", 2, x < columns - 1, me + 1)
    left = ("left", 3, x > 0, me - 1)
    along_z, along_x = (up, down), (right, left)

    barrier = pltpu.get_barrier_semaphore()
    expected = jnp.int32(groups - 1)
    for mask in range(1, groups):
        target = flipped(group, mask, groups)
        pl.semaphore_signal(barrier, inc=1, device_id={"chan": target}, device_id_type=MESH)
    for _, _, exists, target in along_z + along_x:
        expected = expected + exists.astype(jnp.int32)

        @pl.when(exists)
        def _(target=target):
            pl.semaphore_signal(barrier, inc=1, device_id={"inp": target}, device_id_type=MESH)

    pl.semaphore_wait(barrier, expected)

    def where(chunk):
        if isinstance(chunk, int) and chunk < 2:
            return 0, chunk * crossed, (channels - crossed if chunk else crossed)
        return 1 + (chunk - 2) // PARTS, (chunk - 2) % PARTS * step, step

    def rows_of(block, first, count, time):
        return all_ref.at[
            block, pl.ds(first, count), pl.ds(pl.multiple_of(time * depth, depth), depth)
        ]

    def part(block, chunk):
        mask, first, count = where(chunk)
        return rows_of(block, first, count, flipped(group, mask, groups))

    def own_part(chunk):
        mask, first, count = where(chunk)
        return own_ref.at[pl.ds(flipped(group, mask, groups) * channels + first, count)]

    def turn(chunk, arriving=False):
        mask, first, count = where(chunk)
        return pltpu.make_async_remote_copy(
            src_ref=own_part(chunk),
            dst_ref=part(me, chunk) if arriving else rows_of(me, first, count, group),
            send_sem=turn_send.at[chunk],
            recv_sem=turn_recv.at[chunk],
            device_id={"chan": flipped(group, mask, groups)},
            device_id_type=MESH,
        )

    def copy(block, chunk, way, to_sems, source=None):
        place = part(block, chunk)
        return pltpu.make_async_remote_copy(
            src_ref=place if source is None else source,
            dst_ref=place,
            send_sem=to_sems.at[way[1], block],
            recv_sem=recv_sem.at[block, chunk],
            device_id={"inp": way[3]},
            device_id_type=MESH,
        )

    def send(block, chunk, ways, to_sems, source=None):
        for way in ways:

            @pl.when(way[2])
            def _(way=way):
                copy(block, chunk, way, to_sems, source).start()

    def pass_on(block, chunk, exists, ways, to_sems, origin):
        @pl.when(exists)
        def _():
            copy(block, chunk, origin, to_sems).wait_recv()
            send(block, chunk, ways, to_sems)

    def over(first, last, body):
        def one(chunk, carry):
            body(chunk)
            return carry

        for chunk in range(first, min(last, 2)):
            body(chunk)
        if last > 2:
            lax.fori_loop(max(first, 2), last, one, jnp.int32(0))

    def of_mask(mask):
        return (1, 2) if mask == 0 else (2 + (mask - 1) * PARTS, 2 + mask * PARTS)

    over(2, chunks, lambda c: turn(c).start())
    send(me, 0, along_x + along_z, send_cross, own_part(0))
    send(me, 1, along_z + along_x, send_line, own_part(1))
    load = pltpu.make_async_copy(own_ref.at[pl.ds(group * channels, channels)], stage, local_sem.at[0])
    load.start()
    load.wait()
    store = pltpu.make_async_copy(
        stage,
        all_ref.at[me, :, pl.ds(pl.multiple_of(group * depth, depth), depth)],
        local_sem.at[1],
    )
    store.start()

    def own_turned(mask):
        def one(chunk):
            turn(chunk, True).wait_recv()
            send(me, chunk, along_z + along_x, send_line)

        over(*of_mask(mask), one)

    def line(away, first, last):
        below, above = z >= away, z + away < rows

        def one(chunk):
            pass_on(me - away * columns, chunk, below, along_x + (up,), send_line, down)
            pass_on(me + away * columns, chunk, above, along_x + (down,), send_line, up)

        over(first, last, one)

    def crossing(away):
        below, above = z >= away, z + away < rows
        for column in range(columns):
            low = (z - away) * columns + column
            high = (z + away) * columns + column
            pass_on(low, 0, below, (up,), send_cross, down)
            pass_on(high, 0, above, (down,), send_cross, up)

    for away in range(1, columns):
        pass_on(me - away, 0, x >= away, (right,) + along_z, send_cross, left)
        pass_on(me + away, 0, x + away < columns, (left,) + along_z, send_cross, right)
    own_turned(1)
    crossing(1)
    line(1, *of_mask(0))
    for mask in range(2, groups):
        own_turned(mask)
        line(1, *of_mask(mask - 1))
    line(1, *of_mask(groups - 1))
    for away in range(2, rows):
        crossing(away)
        line(away, 1, chunks)
    for away in range(1, columns):
        for row in range(rows):
            before = row * columns + x - away
            after = row * columns + x + away

            def across(chunk):
                pass_on(before, chunk, x >= away, (right,), send_line, left)
                pass_on(after, chunk, x + away < columns, (left,), send_line, right)

            over(1, chunks, across)

    def drain(block, way, cond, to_sems, count):
        @pl.when(jnp.logical_and(cond, way[2]))
        def _():
            whole = all_ref.at[block, pl.ds(0, count)]
            pltpu.make_async_remote_copy(
                src_ref=whole,
                dst_ref=whole,
                send_sem=to_sems.at[way[1], block],
                recv_sem=recv_sem.at[block, 0],
                device_id={"inp": way[3]},
                device_id_type=MESH,
            ).wait_send()

    for row in range(rows):
        for column in range(columns):
            block = row * columns + column
            here, same = x == column, z == row
            drain(block, up, jnp.logical_and(here, z >= row), send_line, channels - crossed // groups)
            drain(block, down, jnp.logical_and(here, z <= row), send_line, channels - crossed // groups)
            drain(block, right, x >= column, send_line, channels - crossed // groups)
            drain(block, left, x <= column, send_line, channels - crossed // groups)
            drain(block, up, z >= row, send_cross, crossed // groups)
            drain(block, down, z <= row, send_cross, crossed // groups)
            drain(block, right, jnp.logical_and(same, x >= column), send_cross, crossed // groups)
            drain(block, left, jnp.logical_and(same, x <= column), send_cross, crossed // groups)
    over(2, chunks, lambda c: turn(c).wait_send())
    store.wait()


def gather(spectra):
    devices, groups = lax.axis_size("inp"), lax.axis_size("chan")
    columns = 1 << (int(math.log2(devices)) // 2)
    rows = devices // columns
    channels, depth, width = spectra.shape[0] // groups, spectra.shape[1], spectra.shape[2]
    chunks = 2 + (groups - 1) * PARTS
    share = ((columns - 1) * rows - rows + 1) / (2 * (rows - 1) * (columns - 1))
    crossed = min(int(0.94 * share * groups * channels), channels - 16) // 16 * 16
    return pl.pallas_call(
        functools.partial(gather_kernel, (rows, columns, groups, crossed)),
        out_shape=jax.ShapeDtypeStruct((devices, channels, groups * depth, width), spectra.dtype),
        in_specs=[pl.BlockSpec(memory_space=pl.ANY)],
        out_specs=pl.BlockSpec(memory_space=pl.ANY),
        scratch_shapes=[
            pltpu.VMEM((channels, depth, width), spectra.dtype),
            pltpu.SemaphoreType.DMA((4, devices)),
            pltpu.SemaphoreType.DMA((4, devices)),
            pltpu.SemaphoreType.DMA((devices, chunks)),
            pltpu.SemaphoreType.DMA((chunks,)),
            pltpu.SemaphoreType.DMA((chunks,)),
            pltpu.SemaphoreType.DMA((2,)),
        ],
        compiler_params=pltpu.CompilerParams(
            collective_id=0, has_side_effects=True, vmem_limit_bytes=4 << 20
        ),
        name="gather",
    )(spectra)


def tile_kernel(slots, frames, groups, table_ref, all_ref, out_ref):
    depth = all_ref.shape[2]
    local = depth // (2 * groups)

    def scaled(block, channel):
        rows = all_ref[block, channel].astype(jnp.float32)
        autopower = jnp.sum(rows * rows, axis=0, keepdims=True) / frames + 1e-06
        return rows * (1.0 / (math.sqrt(frames) * jnp.sqrt(autopower)))

    def one(channel, carry):
        for slot in range(slots):
            first, second = table_ref[slot, 0], table_ref[slot, 1]
            left = scaled(jnp.maximum(first, 0), channel)
            left = jnp.where(first >= 0, left, jnp.zeros_like(left)).astype(jnp.bfloat16)
            right = scaled(jnp.maximum(second, 0), channel).astype(jnp.bfloat16)
            pieces = []
            for start in range(0, depth, 2 * local):
                pieces.append(-right[start + local : start + 2 * local])
                pieces.append(right[start : start + local])
            partner = jnp.concatenate([right, jnp.concatenate(pieces, axis=0)], axis=1)
            out_ref[channel, slot] = lax.dot_general(
                left, partner, (((0,), (0,)), ((), ())), preferred_element_type=jnp.float32
            )
        return carry

    lax.fori_loop(0, all_ref.shape[1], one, jnp.int32(0), unroll=2)


def make_tiles(everything, slot_rows):
    devices, channel_count, depth, width = everything.shape
    slots = slot_rows.shape[0]
    group = 8
    return pl.pallas_call(
        functools.partial(tile_kernel, slots, depth // 2, lax.axis_size("chan")),
        out_shape=jax.ShapeDtypeStruct((channel_count, slots, width, 2 * width), jnp.float32),
        grid_spec=pltpu.PrefetchScalarGridSpec(
            num_scalar_prefetch=1,
            grid=(channel_count // group,),
            in_specs=[pl.BlockSpec((devices, group, depth, width), lambda c, t: (0, c, 0, 0))],
            out_specs=pl.BlockSpec((group, slots, width, 2 * width), lambda c, t: (c, 0, 0, 0)),
        ),
        compiler_params=pltpu.CompilerParams(vmem_limit_bytes=24 << 20),
        name="tiles",
    )(slot_rows, everything)


def on_device(voltages, tile_table):
    everything = gather(channelize(voltages))
    slot_total = tile_table.shape[0] // lax.axis_size("inp")
    slot_rows = lax.dynamic_slice_in_dim(
        tile_table, lax.axis_index("inp") * slot_total, slot_total, 0
    )
    return make_tiles(everything, slot_rows)


def solution(mesh):
    placed = (P("inp", "chan"), P())
    return jax.shard_map(
        on_device,
        mesh=mesh,
        in_specs=placed,
        out_specs=P("chan", "inp", None, None),
        check_vma=False,
    )
```

```python
import functools
import math

import jax
import jax.numpy as jnp
from jax import lax
from jax.experimental import pallas as pl
from jax.experimental.pallas import tpu as pltpu
from jax.sharding import PartitionSpec as P

L = 2048
NCH = 512
TAPS = 4
FINE = 128
PAIR = 2
MESH = pl.DeviceIdType.MESH


def filter_window():
    positions = jnp.arange(TAPS * L, dtype=jnp.float32)
    shape_sinc = jnp.sinc((positions - TAPS * L / 2.0) / L)
    tapering = 0.5 - 0.5 * jnp.cos(2.0 * math.pi * positions / (TAPS * L))
    return (shape_sinc * tapering).reshape(TAPS, L)


def turn_angles(rows, samples, quarter):
    channels, parts = rows // 2, rows % 2
    phases = (channels[:, None] * samples[None, :] + quarter * parts[:, None]) % L
    angles = phases.astype(jnp.float32) * (2.0 * math.pi / L)
    return jnp.cos(angles), jnp.sin(angles)


def table_factors():
    rows = jnp.arange(2 * NCH, dtype=jnp.int32)
    coarse = turn_angles(rows, jnp.arange(L // FINE, dtype=jnp.int32) * FINE, 0)
    fine = turn_angles(rows, jnp.arange(L, dtype=jnp.int32)[:FINE], L // 4)
    return coarse + fine


def fill_table(factors, table):
    coarse_cos, coarse_sin, fine_cos, fine_sin = factors
    strip = 128

    def one(index, carry):
        rows = pl.ds(pl.multiple_of(index * strip, strip), strip)
        cosines, sines = fine_cos[rows, :], fine_sin[rows, :]
        for column in range(L // FINE):
            table[rows, column * FINE : (column + 1) * FINE] = (
                coarse_cos[rows, column : column + 1] * cosines
                - coarse_sin[rows, column : column + 1] * sines
            ).astype(jnp.bfloat16)
        return carry

    lax.fori_loop(0, table.shape[0] // strip, one, jnp.int32(0))


def channel_kernel(groups, volt_ref, *refs):
    factors, window_ref, out_ref, scratch = refs[:4], refs[4], refs[5], refs[6:]
    extended, filtered, table_ref, total, load_sem, send_sem, recv_sem = scratch
    width, local_len = volt_ref.shape
    frames = local_len // L
    halo_len = (TAPS - 1) * L
    me = lax.axis_index("chan")
    has_next, has_last = me < groups - 1, me > 0

    load = pltpu.make_async_copy(volt_ref, extended.at[:, pl.ds(0, local_len)], load_sem)
    load.start()
    barrier = pltpu.get_barrier_semaphore()
    for exists, target in ((has_next, me + 1), (has_last, me - 1)):

        @pl.when(exists)
        def _(target=target):
            pl.semaphore_signal(barrier, inc=1, device_id={"chan": target}, device_id_type=MESH)

    pl.semaphore_wait(barrier, has_next.astype(jnp.int32) + has_last.astype(jnp.int32))
    halo = pltpu.make_async_remote_copy(
        src_ref=volt_ref.at[:, pl.ds(0, halo_len)],
        dst_ref=extended.at[:, pl.ds(local_len, halo_len)],
        send_sem=send_sem,
        recv_sem=recv_sem,
        device_id={"chan": me - 1},
        device_id_type=MESH,
    )

    @pl.when(has_last)
    def _():
        halo.start()

    @pl.when(jnp.logical_not(has_next))
    def _():
        extended[:, pl.ds(local_len, halo_len)] = jnp.zeros((width, halo_len), jnp.bfloat16)

    fill_table(factors, table_ref)
    load.wait()
    strip, lanes = 16, 512

    def one_pair(pair):
        for inner in range(PAIR):
            frame = pair * PAIR + inner
            for first in range(0, L, lanes):
                weights = [
                    window_ref[tap : tap + 1, first : first + lanes] for tap in range(TAPS)
                ]

                def one_strip(index, carry):
                    rows = pl.ds(pl.multiple_of(index * strip, strip), strip)
                    value = jnp.zeros((strip, lanes), jnp.float32)
                    for tap in range(TAPS):
                        start = pl.multiple_of((frame + tap) * L + first, 128)
                        value = value + (
                            extended[rows, pl.ds(start, lanes)].astype(jnp.float32) * weights[tap]
                        )
                    to = pl.ds(pl.multiple_of(inner * width + index * strip, strip), strip)
                    filtered[to, first : first + lanes] = value.astype(jnp.bfloat16)
                    return carry

                lax.fori_loop(0, width // strip, one_strip, jnp.int32(0), unroll=2)
        step = min(256, 2 * NCH)
        for row in range(0, 2 * NCH, step):
            product = lax.dot_general(
                table_ref[row : row + step, :],
                filtered[...],
                (((1,), (1,)), ((), ())),
                preferred_element_type=jnp.float32,
            )
            for inner in range(PAIR):
                where = pl.ds(row * frames + pair * PAIR + inner, step, stride=frames)
                total[where, :] = product[:, inner * width : (inner + 1) * width]

    def pairs(first, last):
        def one(pair, carry):
            one_pair(pair)
            return carry

        lax.fori_loop(first, last, one, jnp.int32(0))

    clear = max(0, (frames - TAPS + 1) // PAIR)
    pairs(0, clear)

    @pl.when(has_next)
    def _():
        halo.wait_recv()

    pairs(clear, frames // PAIR)

    def put(index, carry):
        rows = pl.ds(pl.multiple_of(index * 256, 256), 256)
        out_ref[rows, :] = total[rows, :].astype(jnp.bfloat16)
        return carry

    lax.fori_loop(0, out_ref.shape[0] // 256, put, jnp.int32(0))

    @pl.when(has_last)
    def _():
        halo.wait_send()


def channelize(voltages):
    width, local_len = voltages.shape
    frames = local_len // L
    in_vmem = pl.BlockSpec(memory_space=pltpu.VMEM)
    spectra = pl.pallas_call(
        functools.partial(channel_kernel, lax.axis_size("chan")),
        out_shape=jax.ShapeDtypeStruct((2 * NCH * frames, width), jnp.bfloat16),
        in_specs=[pl.BlockSpec(memory_space=pl.ANY)] + [in_vmem] * 5,
        out_specs=in_vmem,
        scratch_shapes=[
            pltpu.VMEM((width, local_len + (TAPS - 1) * L), jnp.bfloat16),
            pltpu.VMEM((PAIR * width, L), jnp.bfloat16),
            pltpu.VMEM((2 * NCH, L), jnp.bfloat16),
            pltpu.VMEM((2 * NCH * frames, width), jnp.float32),
            pltpu.SemaphoreType.DMA,
            pltpu.SemaphoreType.DMA,
            pltpu.SemaphoreType.DMA,
        ],
        compiler_params=pltpu.CompilerParams(
            collective_id=1, has_side_effects=True, vmem_limit_bytes=56 << 20
        ),
        name="channels",
    )(voltages, *table_factors(), filter_window())
    return spectra.reshape(NCH, 2 * frames, width)


def flipped(group, mask, groups):
    result, bit = group, 1
    while bit < groups:
        result = result + (mask // bit % 2) * bit * (1 - 2 * (group // bit % 2))
        bit *= 2
    return result


PARTS = 2


def gather_kernel(sizes, own_ref, all_ref, stage, *sems):
    rows, columns, groups, crossed = sizes
    send_line, send_cross, recv_sem, turn_send, turn_recv, local_sem = sems
    channels, depth = own_ref.shape[0] // groups, own_ref.shape[1]
    step = channels // PARTS
    chunks = 2 + (groups - 1) * PARTS
    me, group = lax.axis_index("inp"), lax.axis_index("chan")
    z, x = me // columns, me % columns
    up = ("up", 0, z < rows - 1, me + columns)
    down = ("down", 1, z > 0, me - columns)
    right = ("right", 2, x < columns - 1, me + 1)
    left = ("left", 3, x > 0, me - 1)
    along_z, along_x = (up, down), (right, left)

    barrier = pltpu.get_barrier_semaphore()
    expected = jnp.int32(groups - 1)
    for mask in range(1, groups):
        target = flipped(group, mask, groups)
        pl.semaphore_signal(barrier, inc=1, device_id={"chan": target}, device_id_type=MESH)
    for _, _, exists, target in along_z + along_x:
        expected = expected + exists.astype(jnp.int32)

        @pl.when(exists)
        def _(target=target):
            pl.semaphore_signal(barrier, inc=1, device_id={"inp": target}, device_id_type=MESH)

    pl.semaphore_wait(barrier, expected)

    def where(chunk):
        if isinstance(chunk, int) and chunk < 2:
            return 0, chunk * crossed, (channels - crossed if chunk else crossed)
        return 1 + (chunk - 2) // PARTS, (chunk - 2) % PARTS * step, step

    def rows_of(block, first, count, time):
        return all_ref.at[
            block, pl.ds(first, count), pl.ds(pl.multiple_of(time * depth, depth), depth)
        ]

    def part(block, chunk):
        mask, first, count = where(chunk)
        return rows_of(block, first, count, flipped(group, mask, groups))

    def own_part(chunk):
        mask, first, count = where(chunk)
        return own_ref.at[pl.ds(flipped(group, mask, groups) * channels + first, count)]

    def turn(chunk, arriving=False):
        mask, first, count = where(chunk)
        return pltpu.make_async_remote_copy(
            src_ref=own_part(chunk),
            dst_ref=part(me, chunk) if arriving else rows_of(me, first, count, group),
            send_sem=turn_send.at[chunk],
            recv_sem=turn_recv.at[chunk],
            device_id={"chan": flipped(group, mask, groups)},
            device_id_type=MESH,
        )

    def copy(block, chunk, way, to_sems, source=None):
        place = part(block, chunk)
        return pltpu.make_async_remote_copy(
            src_ref=place if source is None else source,
            dst_ref=place,
            send_sem=to_sems.at[way[1], block],
            recv_sem=recv_sem.at[block, chunk],
            device_id={"inp": way[3]},
            device_id_type=MESH,
        )

    def send(block, chunk, ways, to_sems, source=None):
        for way in ways:

            @pl.when(way[2])
            def _(way=way):
                copy(block, chunk, way, to_sems, source).start()

    def pass_on(block, chunk, exists, ways, to_sems, origin):
        @pl.when(exists)
        def _():
            copy(block, chunk, origin, to_sems).wait_recv()
            send(block, chunk, ways, to_sems)

    def over(first, last, body):
        def one(chunk, carry):
            body(chunk)
            return carry

        for chunk in range(first, min(last, 2)):
            body(chunk)
        if last > 2:
            lax.fori_loop(max(first, 2), last, one, jnp.int32(0))

    def of_mask(mask):
        return (1, 2) if mask == 0 else (2 + (mask - 1) * PARTS, 2 + mask * PARTS)

    over(2, chunks, lambda c: turn(c).start())
    send(me, 0, along_x + along_z, send_cross, own_part(0))
    send(me, 1, along_z + along_x, send_line, own_part(1))
    load = pltpu.make_async_copy(own_ref.at[pl.ds(group * channels, channels)], stage, local_sem.at[0])
    load.start()
    load.wait()
    store = pltpu.make_async_copy(
        stage,
        all_ref.at[me, :, pl.ds(pl.multiple_of(group * depth, depth), depth)],
        local_sem.at[1],
    )
    store.start()

    def own_turned(mask):
        def one(chunk):
            turn(chunk, True).wait_recv()
            send(me, chunk, along_z + along_x, send_line)

        over(*of_mask(mask), one)

    def line(away, first, last):
        below, above = z >= away, z + away < rows

        def one(chunk):
            pass_on(me - away * columns, chunk, below, along_x + (up,), send_line, down)
            pass_on(me + away * columns, chunk, above, along_x + (down,), send_line, up)

        over(first, last, one)

    def crossing(away):
        below, above = z >= away, z + away < rows
        for column in range(columns):
            low = (z - away) * columns + column
            high = (z + away) * columns + column
            pass_on(low, 0, below, (up,), send_cross, down)
            pass_on(high, 0, above, (down,), send_cross, up)

    for away in range(1, columns):
        pass_on(me - away, 0, x >= away, (right,) + along_z, send_cross, left)
        pass_on(me + away, 0, x + away < columns, (left,) + along_z, send_cross, right)
    own_turned(1)
    crossing(1)
    line(1, *of_mask(0))
    for mask in range(2, groups):
        own_turned(mask)
        line(1, *of_mask(mask - 1))
    line(1, *of_mask(groups - 1))
    for away in range(2, rows):
        crossing(away)
        line(away, 1, chunks)
    for away in range(1, columns):
        for row in range(rows):
            before = row * columns + x - away
            after = row * columns + x + away

            def across(chunk):
                pass_on(before, chunk, x >= away, (right,), send_line, left)
                pass_on(after, chunk, x + away < columns, (left,), send_line, right)

            over(1, chunks, across)

    def drain(block, way, cond, to_sems, count):
        @pl.when(jnp.logical_and(cond, way[2]))
        def _():
            whole = all_ref.at[block, pl.ds(0, count)]
            pltpu.make_async_remote_copy(
                src_ref=whole,
                dst_ref=whole,
                send_sem=to_sems.at[way[1], block],
                recv_sem=recv_sem.at[block, 0],
                device_id={"inp": way[3]},
                device_id_type=MESH,
            ).wait_send()

    for row in range(rows):
        for column in range(columns):
            block = row * columns + column
            here, same = x == column, z == row
            drain(block, up, jnp.logical_and(here, z >= row), send_line, channels - crossed // groups)
            drain(block, down, jnp.logical_and(here, z <= row), send_line, channels - crossed // groups)
            drain(block, right, x >= column, send_line, channels - crossed // groups)
            drain(block, left, x <= column, send_line, channels - crossed // groups)
            drain(block, up, z >= row, send_cross, crossed // groups)
            drain(block, down, z <= row, send_cross, crossed // groups)
            drain(block, right, jnp.logical_and(same, x >= column), send_cross, crossed // groups)
            drain(block, left, jnp.logical_and(same, x <= column), send_cross, crossed // groups)
    over(2, chunks, lambda c: turn(c).wait_send())
    store.wait()


def gather(spectra):
    devices, groups = lax.axis_size("inp"), lax.axis_size("chan")
    columns = 1 << (int(math.log2(devices)) // 2)
    rows = devices // columns
    channels, depth, width = spectra.shape[0] // groups, spectra.shape[1], spectra.shape[2]
    chunks = 2 + (groups - 1) * PARTS
    share = ((columns - 1) * rows - rows + 1) / (2 * (rows - 1) * (columns - 1))
    crossed = min(int(0.94 * share * groups * channels), channels - 16) // 16 * 16
    return pl.pallas_call(
        functools.partial(gather_kernel, (rows, columns, groups, crossed)),
        out_shape=jax.ShapeDtypeStruct((devices, channels, groups * depth, width), spectra.dtype),
        in_specs=[pl.BlockSpec(memory_space=pl.ANY)],
        out_specs=pl.BlockSpec(memory_space=pl.ANY),
        scratch_shapes=[
            pltpu.VMEM((channels, depth, width), spectra.dtype),
            pltpu.SemaphoreType.DMA((4, devices)),
            pltpu.SemaphoreType.DMA((4, devices)),
            pltpu.SemaphoreType.DMA((devices, chunks)),
            pltpu.SemaphoreType.DMA((chunks,)),
            pltpu.SemaphoreType.DMA((chunks,)),
            pltpu.SemaphoreType.DMA((2,)),
        ],
        compiler_params=pltpu.CompilerParams(
            collective_id=0, has_side_effects=True, vmem_limit_bytes=4 << 20
        ),
        name="gather",
    )(spectra)


def tile_kernel(slots, frames, groups, table_ref, all_ref, out_ref):
    depth = all_ref.shape[2]
    local = depth // (2 * groups)

    def scaled(block, channel):
        rows = all_ref[block, channel].astype(jnp.float32)
        autopower = jnp.sum(rows * rows, axis=0, keepdims=True) / frames + 1e-06
        return rows * (1.0 / (math.sqrt(frames) * jnp.sqrt(autopower)))

    def one(channel, carry):
        for slot in range(slots):
            first, second = table_ref[slot, 0], table_ref[slot, 1]
            left = scaled(jnp.maximum(first, 0), channel)
            left = jnp.where(first >= 0, left, jnp.zeros_like(left)).astype(jnp.bfloat16)
            right = scaled(jnp.maximum(second, 0), channel).astype(jnp.bfloat16)
            pieces = []
            for start in range(0, depth, 2 * local):
                pieces.append(-right[start + local : start + 2 * local])
                pieces.append(right[start : start + local])
            partner = jnp.concatenate([right, jnp.concatenate(pieces, axis=0)], axis=1)
            out_ref[channel, slot] = lax.dot_general(
                left, partner, (((0,), (0,)), ((), ())), preferred_element_type=jnp.float32
            )
        return carry

    lax.fori_loop(0, all_ref.shape[1], one, jnp.int32(0), unroll=2)


def make_tiles(everything, slot_rows):
    devices, channel_count, depth, width = everything.shape
    slots = slot_rows.shape[0]
    lanes = max(width, 128)
    block_bytes = 2 * devices * depth * lanes + 4 * slots * width * max(2 * width, 128)
    group = 8
    while 2 * group * block_bytes > 16 << 20:
        group //= 2
    return pl.pallas_call(
        functools.partial(tile_kernel, slots, depth // 2, lax.axis_size("chan")),
        out_shape=jax.ShapeDtypeStruct((channel_count, slots, width, 2 * width), jnp.float32),
        grid_spec=pltpu.PrefetchScalarGridSpec(
            num_scalar_prefetch=1,
            grid=(channel_count // group,),
            in_specs=[pl.BlockSpec((devices, group, depth, width), lambda c, t: (0, c, 0, 0))],
            out_specs=pl.BlockSpec((group, slots, width, 2 * width), lambda c, t: (c, 0, 0, 0)),
        ),
        compiler_params=pltpu.CompilerParams(vmem_limit_bytes=20 << 20),
        name="tiles",
    )(slot_rows, everything)


def on_device(voltages, tile_table):
    everything = gather(channelize(voltages))
    slot_total = tile_table.shape[0] // lax.axis_size("inp")
    slot_rows = lax.dynamic_slice_in_dim(
        tile_table, lax.axis_index("inp") * slot_total, slot_total, 0
    )
    return make_tiles(everything, slot_rows)


def solution(mesh):
    placed = (P("inp", "chan"), P())
    return jax.shard_map(
        on_device,
        mesh=mesh,
        in_specs=placed,
        out_specs=P("chan", "inp", None, None),
        check_vma=False,
    )
```
